32 devices in a mesh: shard: 4 (over y, x), ctx: 4 (over z), tp: 2 (over core).
Axes of the slice: x: 2, y: 2, z: 4, core: 2. Of those that a mesh axis runs over, the one named last changes fastest.
Arguments:
- inputs: bfloat16 [4096, 1024], P(('shard', 'ctx')), may hold values from -6 to 6
- lengths: int32 [4, 3], P('shard'), may hold values from 1 to 768, 1024 in all within a row
- cotangent: bfloat16 [4096, 1024], P(('shard', 'ctx')), may hold values from -6 to 6
- w_qkv: bfloat16 [3, 1024, 1024], P(None, 'shard', 'tp'), may hold values from -0.1875 to 0.1875
- w_out: bfloat16 [1024, 1024], P('tp', 'shard'), may hold values from -0.5 to 0.5
- w_fc: bfloat16 [1024, 4096], P('shard', 'tp'), may hold values from -0.1875 to 0.1875
- w_proj: bfloat16 [4096, 1024], P('tp', 'shard'), may hold values from -0.09375 to 0.09375
- b_qv: float32 [2, 1024], P(None, 'tp'), may hold values from -3 to 3
- b_out: float32 [1024], replicated, may hold values from -2 to 2
- b_fc: float32 [4096], P('tp'), may hold values from -3 to 3
- b_proj: float32 [1024], replicated, may hold values from -2 to 2
- ln1_gain: float32 [1024], replicated, may hold values from 0.25 to 1.75
- ln1_bias: float32 [1024], replicated, may hold values from -2 to 2
- ln2_gain: float32 [1024], replicated, may hold values from 0.25 to 1.75
- ln2_bias: float32 [1024], replicated, may hold values from -2 to 2
Outputs:
- outputs: bfloat16 [4096, 1024], P(('shard', 'ctx'))
- grad_inputs: bfloat16 [4096, 1024], P(('shard', 'ctx'))
- grad_w_qkv: float32 [3, 1024, 1024], P(None, 'shard', 'tp')
- grad_w_out: float32 [1024, 1024], P('tp', 'shard')
- grad_w_fc: float32 [1024, 4096], P('shard', 'tp')
- grad_w_proj: float32 [4096, 1024], P('tp', 'shard')
- grad_b_qv: float32 [2, 1024], P(None, 'tp')
- grad_b_out: float32 [1024], replicated
- grad_b_fc: float32 [4096], P('tp')
- grad_b_proj: float32 [1024], replicated
- grad_ln1_gain: float32 [1024], replicated
- grad_ln1_bias: float32 [1024], replicated
- grad_ln2_gain: float32 [1024], replicated
- grad_ln2_bias: float32 [1024], replicated
The draws below stay inside these ranges and needn't reach their ends.
Inputs may be any that keep to these rules, and one draw needn't show every extreme that they name: Each row holds the lengths of one shard's 3 sequences in order; they sum to 1024, and the largest is 768.
All inputs are finite; a program needn't handle non-finite values.
Results may differ from the reference program's by a relative error of at most 0.02.
Values may be sent and summed in bfloat16 or wider, within the bound.
A program may use at most 128 MiB of HBM per device.

```python
import math
import jax
import jax.numpy as jnp
import numpy as np
from jax import lax

D = 1024
HEADS = 16
HEAD_DIM = 64
FF = 4096
SEQS = 3
BLOCK = 1024
SEQ_MOST = 768
SHARDS = 4
TOKENS = 4096


def shard_levels(stream_key, dims, cuts, least, largest):
    factor_of, own = 1.0, jax.random.fold_in(stream_key, 6)
    for dim, parts in cuts:
        heights = jnp.exp(jax.random.uniform(jax.random.fold_in(own, dim), (parts,), jnp.float32, least / len(cuts), largest / len(cuts)))
        factor_of = factor_of * jnp.repeat(heights, dims[dim] // parts).reshape([-1 if axis == dim else 1 for axis in range(len(dims))])
    return factor_of


def length_profile(count, total, reach, slope):
    loads = [(1 << 20) // math.isqrt(rank ** slope) + 1 for rank in range(2, count + 1)]
    surplus, holding = total - reach - (count - 1), [1] * (count - 1)
    while surplus > 0:
        movable = [i for i in range(count - 1) if holding[i] < reach]
        mass, remaining = sum([loads[i] for i in movable]), surplus
        for i in movable:
            addition = min(reach - holding[i], max(1, remaining * loads[i] // mass), surplus)
            holding[i] = holding[i] + addition
            surplus = surplus - addition
    return np.array([reach] + holding)


def uneven_parts(rng, amount, total, reach, skew):
    if amount == 2:
        one = jax.random.randint(rng, (), max(1, total - reach), min(reach, total - 1) + 1)
        return jnp.stack([one, total - one])
    tallies = jnp.asarray(length_profile(amount, total, reach, skew), jnp.int32)
    pairs = (amount - 1) // 2
    donor, sink = tallies[1:1 + 2 * pairs:2], tallies[2:2 + 2 * pairs:2]
    slack = jnp.minimum(donor - 1, reach - sink)
    passed = jax.random.randint(jax.random.fold_in(rng, 1), (pairs,), 0, 1 << 20) % (slack + 1)
    tallies = tallies.at[1:1 + 2 * pairs:2].set(donor - passed).at[2:2 + 2 * pairs:2].set(sink + passed)
    return tallies[jax.random.permutation(jax.random.fold_in(rng, 2), amount)]


def noise(key, dims, deviation, limit, shards=(), held_as=jnp.bfloat16):
    result = jax.random.normal(key, dims, jnp.float32) * deviation
    if len(shards) > 0:
        result = shard_levels(key, dims, shards, -0.22, 0.18) * result
    return jnp.clip(result, min=-limit, max=limit).astype(held_as)


def setup_inputs(seed: int = 0) -> dict:
    splits = jax.random.split(jax.random.key(seed), 16)
    inputs = noise(splits[0], (TOKENS, D), 1.0, 6.0, ((0, 16),))
    lengths = jax.vmap(lambda own: uneven_parts(own, SEQS, BLOCK, SEQ_MOST, 2))(jax.random.split(splits[1], SHARDS)).reshape((SHARDS, SEQS)).astype(jnp.int32)
    cotangent = noise(splits[2], (TOKENS, D), 1.0, 6.0, ((0, 16),))
    w_qkv = noise(splits[3], (3, D, D), D ** -0.5, 0.1875, ((1, 4), (2, 2)))
    w_out = noise(splits[4], (D, D), (D // 8) ** -0.5, 0.5, ((0, 2), (1, 4)))
    w_fc = noise(splits[5], (D, FF), D ** -0.5, 0.1875, ((0, 4), (1, 2)))
    w_proj = noise(splits[6], (FF, D), FF ** -0.5, 0.09375, ((0, 2), (1, 4)))
    b_qv = noise(splits[7], (2, D), 0.5, 3.0, ((1, 2),), jnp.float32)
    b_out = noise(splits[8], (D,), 0.3, 2.0, (), jnp.float32)
    b_fc = noise(splits[9], (FF,), 0.5, 3.0, ((0, 2),), jnp.float32)
    b_proj = noise(splits[10], (D,), 0.3, 2.0, (), jnp.float32)
    ln1_gain = jnp.clip(1.0 + 0.15 * jax.random.normal(splits[11], (D,), jnp.float32), 0.25, 1.75)
    ln1_bias = noise(splits[12], (D,), 0.3, 2.0, (), jnp.float32)
    ln2_gain = jnp.clip(1.0 + 0.15 * jax.random.normal(splits[13], (D,), jnp.float32), 0.25, 1.75)
    ln2_bias = noise(splits[14], (D,), 0.3, 2.0, (), jnp.float32)
    return dict(inputs=inputs, lengths=lengths, cotangent=cotangent, w_qkv=w_qkv, w_out=w_out, w_fc=w_fc, w_proj=w_proj, b_qv=b_qv, b_out=b_out, b_fc=b_fc, b_proj=b_proj, ln1_gain=ln1_gain, ln1_bias=ln1_bias, ln2_gain=ln2_gain, ln2_bias=ln2_bias)


def layer_norm(values, gain, shift):
    mean = lax.optimization_barrier(jnp.mean(values, axis=-1, keepdims=True))
    centred = values - mean
    spread = lax.optimization_barrier(jnp.mean(centred * centred, axis=-1, keepdims=True))
    return centred * lax.rsqrt(spread + 1e-05) * gain + shift

def gelu_tanh(values):
    return 0.5 * values * (1.0 + jnp.tanh(0.7978845608028654 * (values + 0.044715 * values * values * values)))

def segment_ids(lengths, count):
    ends = jnp.cumsum(lengths).astype(jnp.int32)
    places = jnp.arange(count, dtype=jnp.int32)
    return lax.optimization_barrier(jnp.sum((places[:, None] >= ends[None, :]).astype(jnp.int32), axis=1)).astype(jnp.int32)

def dot32(left, right):
    return jnp.dot(left, right, preferred_element_type=jnp.float32)

def reference(inputs, lengths, cotangent, w_qkv, w_out, w_fc, w_proj, b_qv, b_out, b_fc, b_proj, ln1_gain, ln1_bias, ln2_gain, ln2_bias):
    bf = jnp.bfloat16
    f32 = jnp.float32
    x_all = inputs.reshape(SHARDS, BLOCK, D)
    dy_all = cotangent.reshape(SHARDS, BLOCK, D)

    def group(carry, data):
        x_rows, lens, d_out = data
        seg = segment_ids(lens, BLOCK)
        places = jnp.arange(BLOCK, dtype=jnp.int32)
        allowed = (places[None, :] <= places[:, None]) & (seg[None, :] == seg[:, None])
        x_f = x_rows.astype(f32)
        normed1 = layer_norm(x_f, ln1_gain, ln1_bias).astype(bf)
        query = ((dot32(normed1, w_qkv[0]) + b_qv[0]) * 0.125).astype(bf)
        key = dot32(normed1, w_qkv[1]).astype(bf)
        value = (dot32(normed1, w_qkv[2]) + b_qv[1]).astype(bf)
        q3 = query.reshape(BLOCK, HEADS, HEAD_DIM).astype(f32)
        k3 = key.reshape(BLOCK, HEADS, HEAD_DIM).astype(f32)
        v3 = value.reshape(BLOCK, HEADS, HEAD_DIM).astype(f32)
        scores = jnp.einsum('rhd,nhd->hrn', q3, k3)
        weights = jnp.where(allowed[None], jnp.exp(scores), 0.0)
        total = lax.optimization_barrier(jnp.sum(weights, axis=2))
        log_total = jnp.log(total)
        acc = jnp.einsum('hrn,nhd->hrd', weights.astype(bf).astype(f32), v3)
        attended = (acc / total[:, :, None]).transpose(1, 0, 2).reshape(BLOCK, D).astype(bf)
        hidden = x_f + dot32(attended, w_out) + b_out
        normed2 = layer_norm(hidden, ln2_gain, ln2_bias).astype(bf)
        pre = dot32(normed2, w_fc) + b_fc
        act = gelu_tanh(pre).astype(bf)
        outputs = (hidden + dot32(act, w_proj) + b_proj).astype(bf)
        grad_f = d_out.astype(f32)
        g_bproj = lax.optimization_barrier(jnp.sum(grad_f, axis=0))
        g_proj = dot32(act.T, d_out)
        d_act = dot32(d_out, w_proj.T)
        gelu_back = jax.vjp(gelu_tanh, pre)[1]
        d_pre = gelu_back(d_act)[0]
        g_bfc = lax.optimization_barrier(jnp.sum(d_pre, axis=0))
        d_pre_b = d_pre.astype(bf)
        g_fc = dot32(normed2.T, d_pre_b)
        d_normed2 = dot32(d_pre_b, w_fc.T)
        norm_back2 = jax.vjp(layer_norm, hidden, ln2_gain, ln2_bias)[1]
        d_norm2, g_ln2g, g_ln2b = norm_back2(d_normed2)
        d_hidden = grad_f + d_norm2
        g_bout = lax.optimization_barrier(jnp.sum(d_hidden, axis=0))
        d_hidden_b = d_hidden.astype(bf)
        g_out = dot32(attended.T, d_hidden_b)
        d_attended = dot32(d_hidden_b, w_out.T).astype(bf)
        da3 = d_attended.reshape(BLOCK, HEADS, HEAD_DIM).astype(f32)
        at3 = attended.reshape(BLOCK, HEADS, HEAD_DIM).astype(f32)
        delta = jnp.einsum('rhd,rhd->hr', da3, at3)
        probs = jnp.where(allowed[None], jnp.exp(scores - log_total[:, :, None]), 0.0)
        d_value = jnp.einsum('hrn,rhd->nhd', probs.astype(bf).astype(f32), da3).reshape(BLOCK, D)
        d_probs = jnp.einsum('rhd,nhd->hrn', da3, v3)
        d_scores_b = (probs * (d_probs - delta[:, :, None])).astype(bf).astype(f32)
        d_query = jnp.einsum('hrn,nhd->rhd', d_scores_b, k3).reshape(BLOCK, D) * 0.125
        d_key = jnp.einsum('hrn,rhd->nhd', d_scores_b, q3).reshape(BLOCK, D)
        g_bqv = jnp.stack([lax.optimization_barrier(jnp.sum(d_query, axis=0)), lax.optimization_barrier(jnp.sum(d_value, axis=0))])
        d_query_b = d_query.astype(bf)
        d_key_b = d_key.astype(bf)
        d_value_b = d_value.astype(bf)
        g_qkv = jnp.stack([dot32(normed1.T, d_query_b), dot32(normed1.T, d_key_b), dot32(normed1.T, d_value_b)])
        d_normed1 = dot32(d_query_b, w_qkv[0].T) + dot32(d_key_b, w_qkv[1].T) + dot32(d_value_b, w_qkv[2].T)
        norm_back1 = jax.vjp(layer_norm, x_f, ln1_gain, ln1_bias)[1]
        d_norm1, g_ln1g, g_ln1b = norm_back1(d_normed1)
        grad_inputs = (d_hidden + d_norm1).astype(bf)
        terms = (g_qkv, g_out, g_fc, g_proj, g_bqv, g_bout, g_bfc, g_bproj, g_ln1g, g_ln1b, g_ln2g, g_ln2b)
        carry = tuple((c + t for c, t in zip(carry, terms)))
        return (carry, (outputs, grad_inputs))
    init = (jnp.zeros((3, D, D), f32), jnp.zeros((D, D), f32), jnp.zeros((D, FF), f32), jnp.zeros((FF, D), f32), jnp.zeros((2, D), f32), jnp.zeros((D,), f32), jnp.zeros((FF,), f32), jnp.zeros((D,), f32), jnp.zeros((D,), f32), jnp.zeros((D,), f32), jnp.zeros((D,), f32), jnp.zeros((D,), f32))
    sums, (outs, grads_in) = lax.scan(group, init, (x_all, lengths, dy_all))
    return (outs.reshape(TOKENS, D), grads_in.reshape(TOKENS, D), sums[0], sums[1], sums[2], sums[3], sums[4], sums[5], sums[6], sums[7], sums[8], sums[9], sums[10], sums[11])
```

```python
import jax
import jax.numpy as jnp
from jax import lax
from jax.sharding import PartitionSpec as P

HEAD_DIM = 64


def layer_norm(values, gain, shift):
    mean = jnp.mean(values, axis=-1, keepdims=True)
    centred = values - mean
    spread = jnp.mean(centred * centred, axis=-1, keepdims=True)
    return centred * lax.rsqrt(spread + 1e-05) * gain + shift


def gelu_tanh(values):
    return (
        0.5
        * values
        * (1.0 + jnp.tanh(0.7978845608028654 * (values + 0.044715 * values * values * values)))
    )


def segment_ids(lengths, count):
    ends = jnp.cumsum(lengths)
    places = jnp.arange(count, dtype=jnp.int32)
    return jnp.sum((places[:, None] >= ends[None, :]).astype(jnp.int32), axis=1)


def dot32(left, right):
    return jnp.dot(left, right, preferred_element_type=jnp.float32)


def on_device_general(
    inputs,
    lengths,
    cotangent,
    w_qkv,
    w_out,
    w_fc,
    w_proj,
    b_qv,
    b_out,
    b_fc,
    b_proj,
    ln1_gain,
    ln1_bias,
    ln2_gain,
    ln2_bias,
):
    bf = jnp.bfloat16
    f32 = jnp.float32
    rows = inputs.shape[0]
    parts = lax.axis_size("ctx")
    block = rows * parts
    local_width = b_qv.shape[1]
    local_heads = local_width // HEAD_DIM
    seg_all = segment_ids(lengths[0], block)
    first = lax.axis_index("ctx") * rows
    q_pos = first + jnp.arange(rows, dtype=jnp.int32)
    q_seg = lax.dynamic_slice_in_dim(seg_all, first, rows)
    wq_all, wo_all, wfc_all, wproj_all = (
        lax.all_gather(w_qkv, "shard", axis=1, tiled=True),
        lax.all_gather(w_out, "shard", axis=1, tiled=True),
        lax.all_gather(w_fc, "shard", axis=0, tiled=True),
        lax.all_gather(w_proj, "shard", axis=1, tiled=True),
    )
    x_f = inputs.astype(f32)
    normed1 = layer_norm(x_f, ln1_gain, ln1_bias).astype(bf)
    query = ((dot32(normed1, wq_all[0]) + b_qv[0]) * 0.125).astype(bf)
    key = dot32(normed1, wq_all[1]).astype(bf)
    value = (dot32(normed1, wq_all[2]) + b_qv[1]).astype(bf)
    q3 = query.reshape(rows, local_heads, HEAD_DIM)

    def allowed_for(start, count):
        k_pos = start + jnp.arange(count, dtype=jnp.int32)
        k_seg = lax.dynamic_slice_in_dim(seg_all, start, count)
        return (k_pos[None, :] <= q_pos[:, None]) & (k_seg[None, :] == q_seg[:, None])

    k_piece = lax.all_gather(key, "ctx", axis=0, tiled=True)
    v_piece = lax.all_gather(value, "ctx", axis=0, tiled=True)
    count = k_piece.shape[0]
    allowed = allowed_for(jnp.int32(0), count)
    scores = jnp.einsum(
        "rhd,nhd->hrn",
        q3,
        k_piece.reshape(count, local_heads, HEAD_DIM),
        preferred_element_type=f32,
    )
    weights = jnp.where(allowed[None], jnp.exp(scores), 0.0)
    total = jnp.sum(weights, axis=2)
    acc = jnp.einsum(
        "hrn,nhd->hrd",
        weights.astype(bf),
        v_piece.reshape(count, local_heads, HEAD_DIM),
        preferred_element_type=f32,
    )
    total, acc = (total, acc)
    log_total = jnp.log(total)
    attended = (acc / total[:, :, None]).transpose(1, 0, 2).reshape(rows, local_width).astype(bf)
    mixed = lax.psum(dot32(attended, wo_all).astype(jnp.bfloat16), "tp").astype(jnp.float32)
    hidden = x_f + mixed + b_out
    normed2 = layer_norm(hidden, ln2_gain, ln2_bias).astype(bf)
    pre = dot32(normed2, wfc_all) + b_fc
    act = gelu_tanh(pre).astype(bf)
    mlp_total = lax.psum(dot32(act, wproj_all).astype(jnp.bfloat16), "tp").astype(jnp.float32)
    outputs = (hidden + mlp_total + b_proj).astype(bf)
    wq_back, wo_back, wfc_back, wproj_back = (
        lax.all_gather(w_qkv, "shard", axis=1, tiled=True),
        lax.all_gather(w_out, "shard", axis=1, tiled=True),
        lax.all_gather(w_fc, "shard", axis=0, tiled=True),
        lax.all_gather(w_proj, "shard", axis=1, tiled=True),
    )
    grad_f = cotangent.astype(f32)
    g_bproj = jnp.sum(grad_f, axis=0)
    g_proj = dot32(act.T, cotangent)
    d_act = dot32(cotangent, wproj_back.T)
    gelu_back = jax.vjp(gelu_tanh, pre)[1]
    d_pre = gelu_back(d_act)[0]
    g_bfc = jnp.sum(d_pre, axis=0)
    d_pre_b = d_pre.astype(bf)
    g_fc = dot32(normed2.T, d_pre_b)
    d_normed2 = lax.psum(dot32(d_pre_b, wfc_back.T).astype(jnp.bfloat16), "tp").astype(jnp.float32)
    norm_back2 = jax.vjp(layer_norm, hidden, ln2_gain, ln2_bias)[1]
    d_norm2, g_ln2g, g_ln2b = norm_back2(d_normed2)
    d_hidden = grad_f + d_norm2
    g_bout = jnp.sum(d_hidden, axis=0)
    d_hidden_b = d_hidden.astype(bf)
    g_out = dot32(attended.T, d_hidden_b)
    d_attended = dot32(d_hidden_b, wo_back.T).astype(bf)
    da3 = d_attended.reshape(rows, local_heads, HEAD_DIM)
    at3 = attended.reshape(rows, local_heads, HEAD_DIM)
    delta = jnp.einsum("rhd,rhd->hr", da3, at3, preferred_element_type=f32)
    key_all, value_all = (
        lax.all_gather(key, "ctx", axis=0, tiled=True),
        lax.all_gather(value, "ctx", axis=0, tiled=True),
    )
    key_blocks = key_all.reshape(parts, rows, local_heads, HEAD_DIM)
    value_blocks = value_all.reshape(parts, rows, local_heads, HEAD_DIM)
    starts = jnp.arange(parts, dtype=jnp.int32) * rows

    def back_piece(d_query_acc, inputs_piece):
        k_piece, v_piece, start = inputs_piece
        allowed = allowed_for(start, rows)
        scores = jnp.einsum("rhd,nhd->hrn", q3, k_piece, preferred_element_type=f32)
        probs = jnp.where(allowed[None], jnp.exp(scores - log_total[:, :, None]), 0.0)
        d_v = jnp.einsum("hrn,rhd->nhd", probs.astype(bf), da3, preferred_element_type=f32)
        d_probs = jnp.einsum("rhd,nhd->hrn", da3, v_piece, preferred_element_type=f32)
        d_scores_b = (probs * (d_probs - delta[:, :, None])).astype(bf)
        d_query_acc = d_query_acc + jnp.einsum(
            "hrn,nhd->rhd", d_scores_b, k_piece, preferred_element_type=f32
        )
        d_k = jnp.einsum("hrn,rhd->nhd", d_scores_b, q3, preferred_element_type=f32)
        return (d_query_acc, (d_k.reshape(rows, local_width), d_v.reshape(rows, local_width)))

    zero_query = jnp.zeros((rows, local_heads, HEAD_DIM), f32)
    d_query_acc, (d_key_terms, d_value_terms) = lax.scan(
        back_piece, zero_query, (key_blocks, value_blocks, starts)
    )
    d_key, d_value = (
        lax.psum_scatter(
            d_key_terms.reshape(block, local_width).astype(jnp.bfloat16),
            "ctx",
            scatter_dimension=0,
            tiled=True,
        ).astype(jnp.float32),
        lax.psum_scatter(
            d_value_terms.reshape(block, local_width).astype(jnp.bfloat16),
            "ctx",
            scatter_dimension=0,
            tiled=True,
        ).astype(jnp.float32),
    )
    d_query = d_query_acc.reshape(rows, local_width) * 0.125
    g_bqv = jnp.stack([jnp.sum(d_query, axis=0), jnp.sum(d_value, axis=0)])
    d_query_b = d_query.astype(bf)
    d_key_b = d_key.astype(bf)
    d_value_b = d_value.astype(bf)
    g_qkv = jnp.stack(
        [dot32(normed1.T, d_query_b), dot32(normed1.T, d_key_b), dot32(normed1.T, d_value_b)]
    )
    d_local = (
        dot32(d_query_b, wq_back[0].T)
        + dot32(d_key_b, wq_back[1].T)
        + dot32(d_value_b, wq_back[2].T)
    )
    d_normed1 = lax.psum(d_local.astype(jnp.bfloat16), "tp").astype(jnp.float32)
    norm_back1 = jax.vjp(layer_norm, x_f, ln1_gain, ln1_bias)[1]
    d_norm1, g_ln1g, g_ln1b = norm_back1(d_normed1)
    grad_inputs = (d_hidden + d_norm1).astype(bf)
    part_qkv, part_out, part_fc, part_proj = (
        lax.psum_scatter(
            g_qkv.astype(jnp.bfloat16), "shard", scatter_dimension=1, tiled=True
        ).astype(jnp.float32),
        lax.psum_scatter(
            g_out.astype(jnp.bfloat16), "shard", scatter_dimension=1, tiled=True
        ).astype(jnp.float32),
        lax.psum_scatter(
            g_fc.astype(jnp.bfloat16), "shard", scatter_dimension=0, tiled=True
        ).astype(jnp.float32),
        lax.psum_scatter(
            g_proj.astype(jnp.bfloat16), "shard", scatter_dimension=1, tiled=True
        ).astype(jnp.float32),
    )
    sum_qkv, sum_out, sum_fc, sum_proj = (
        lax.psum(part_qkv.astype(jnp.bfloat16), "ctx").astype(jnp.float32),
        lax.psum(part_out.astype(jnp.bfloat16), "ctx").astype(jnp.float32),
        lax.psum(part_fc.astype(jnp.bfloat16), "ctx").astype(jnp.float32),
        lax.psum(part_proj.astype(jnp.bfloat16), "ctx").astype(jnp.float32),
    )
    small = lax.psum(
        (g_bqv, g_bout, g_bfc, g_bproj, g_ln1g, g_ln1b, g_ln2g, g_ln2b), ("shard", "ctx")
    )
    return (
        outputs,
        grad_inputs,
        sum_qkv,
        sum_out,
        sum_fc,
        sum_proj,
        small[0],
        small[1],
        small[2],
        small[3],
        small[4],
        small[5],
        small[6],
        small[7],
    )


def exchange(pieces_of, place, count, axis):
    me = lax.axis_index(axis)
    arrived = [(me, pieces_of(me))]
    for step in range(1, count):
        pairs = [(i, i ^ step) for i in range(count)]
        arrived.append((me ^ step, lax.ppermute(pieces_of(me ^ step), axis, pairs)))
    return place(arrived)


def all_to_all(values, count, split, concat):
    width = values.shape[split] // count
    depth = values.shape[concat]

    def pieces_of(index):
        return lax.dynamic_slice_in_dim(values, index * width, width, axis=split)

    def place(arrived):
        shape = list(values.shape)
        shape[split] = width
        shape[concat] = depth * count
        result = jnp.zeros(shape, values.dtype)
        for index, piece in arrived:
            result = lax.dynamic_update_slice_in_dim(result, piece, index * depth, axis=concat)
        return result

    return exchange(pieces_of, place, count, "shard")


def plane_gather(values):
    return lax.all_gather(values, ("shard", "tp"), axis=0, tiled=True)


def plane_scatter(values):
    return lax.psum_scatter(
        values.astype(jnp.bfloat16), ("shard", "tp"), scatter_dimension=0, tiled=True
    ).astype(jnp.float32)


def swap_planes(values, count):
    pairs = [(a * count + b, b * count + a) for a in range(count) for b in range(count)]
    return lax.ppermute(values, ("shard", "ctx"), pairs)


def norm_back(values, gain, d_out):
    mean = jnp.mean(values, axis=-1, keepdims=True)
    centred = values - mean
    scale = lax.rsqrt(jnp.mean(centred * centred, axis=-1, keepdims=True) + 1e-05)
    unit = centred * scale
    d_unit = d_out * gain
    first = jnp.mean(d_unit, axis=-1, keepdims=True)
    second = jnp.mean(d_unit * unit, axis=-1, keepdims=True)
    d_values = (d_unit - first - unit * second) * scale
    return d_values, jnp.sum(d_out * unit, axis=0), jnp.sum(d_out, axis=0)


def attention(query, key, value, allowed, heads):
    f32 = jnp.float32
    parts = []
    saved = []
    for head in range(heads):
        cols = slice(head * HEAD_DIM, (head + 1) * HEAD_DIM)
        scores = lax.dot_general(
            query[:, cols], key[:, cols], (((1,), (1,)), ((), ())), preferred_element_type=f32
        )
        weights = jnp.where(allowed, jnp.exp(scores), 0.0)
        total = jnp.sum(weights, axis=1, keepdims=True)
        parts.append(dot32(weights.astype(jnp.bfloat16), value[:, cols]) / total)
        saved.append(jnp.log(total))
    return jnp.concatenate(parts, axis=1).astype(jnp.bfloat16), saved


def attention_back(query, key, value, attended, d_attended, allowed, saved, heads):
    f32 = jnp.float32
    bf = jnp.bfloat16
    d_q, d_k, d_v = [], [], []
    for head in range(heads):
        cols = slice(head * HEAD_DIM, (head + 1) * HEAD_DIM)
        q, k, v, da = query[:, cols], key[:, cols], value[:, cols], d_attended[:, cols]
        delta = jnp.sum(da.astype(f32) * attended[:, cols].astype(f32), axis=1, keepdims=True)
        scores = lax.dot_general(q, k, (((1,), (1,)), ((), ())), preferred_element_type=f32)
        probs = jnp.where(allowed, jnp.exp(scores - saved[head]), 0.0)
        d_v.append(
            lax.dot_general(
                probs.astype(bf), da, (((0,), (0,)), ((), ())), preferred_element_type=f32
            )
        )
        d_probs = lax.dot_general(da, v, (((1,), (1,)), ((), ())), preferred_element_type=f32)
        d_scores = (probs * (d_probs - delta)).astype(bf)
        d_q.append(dot32(d_scores, k))
        d_k.append(
            lax.dot_general(d_scores, q, (((0,), (0,)), ((), ())), preferred_element_type=f32)
        )
    join = lambda items: jnp.concatenate(items, axis=1)
    return join(d_q) * 0.125, join(d_k), join(d_v)


def t_dot(left, right):
    return lax.dot_general(left, right, (((0,), (0,)), ((), ())), preferred_element_type=jnp.float32)


def dot_t(left, right):
    return lax.dot_general(left, right, (((1,), (1,)), ((), ())), preferred_element_type=jnp.float32)


def on_device_plane(
    inputs,
    lengths,
    cotangent,
    w_qkv,
    w_out,
    w_fc,
    w_proj,
    b_qv,
    b_out,
    b_fc,
    b_proj,
    ln1_gain,
    ln1_bias,
    ln2_gain,
    ln2_bias,
):
    bf = jnp.bfloat16
    f32 = jnp.float32
    shards = lax.axis_size("shard")
    cores = lax.axis_size("tp")
    s = lax.axis_index("shard")
    t = lax.axis_index("tp")
    rows = inputs.shape[0] // cores
    block = rows * cores * shards
    model = inputs.shape[1]
    width = b_qv.shape[1] // shards
    heads = width // HEAD_DIM
    units = b_fc.shape[0] // shards
    mine = lambda array: lax.dynamic_slice_in_dim(array, t * rows, rows, axis=0)

    x_f = swap_planes(mine(inputs), shards).astype(f32)
    lens = swap_planes(lengths, shards)[0]
    cot_own = swap_planes(mine(cotangent), shards)
    normed1 = plane_gather(layer_norm(x_f, ln1_gain, ln1_bias).astype(bf))
    wqkv = all_to_all(w_qkv, shards, 2, 1)
    wout = all_to_all(w_out, shards, 0, 1)
    wfc = all_to_all(w_fc, shards, 1, 0)
    wproj = all_to_all(w_proj, shards, 0, 1)
    cot = plane_gather(cot_own)
    b_qv_own = lax.dynamic_slice_in_dim(b_qv, s * width, width, axis=1)
    b_fc_own = lax.dynamic_slice_in_dim(b_fc, s * units, units, axis=0)

    seg = segment_ids(lens, block)
    places = jnp.arange(block, dtype=jnp.int32)
    allowed = (places[None, :] <= places[:, None]) & (seg[None, :] == seg[:, None])

    query = ((dot32(normed1, wqkv[0]) + b_qv_own[0]) * 0.125).astype(bf)
    key = dot32(normed1, wqkv[1]).astype(bf)
    value = (dot32(normed1, wqkv[2]) + b_qv_own[1]).astype(bf)
    attended, saved = attention(query, key, value, allowed, heads)
    hidden = x_f + plane_scatter(dot32(attended, wout)) + b_out
    normed2 = plane_gather(layer_norm(hidden, ln2_gain, ln2_bias).astype(bf))
    pre = dot32(normed2, wfc) + b_fc_own
    act = gelu_tanh(pre).astype(bf)
    d_act = dot_t(cot, wproj)
    d_pre = jax.vjp(gelu_tanh, pre)[1](d_act)[0]
    d_pre_b = d_pre.astype(bf)
    d_normed2 = plane_scatter(dot_t(d_pre_b, wfc))
    mlp_total = plane_scatter(dot32(act, wproj))
    outputs = (hidden + mlp_total + b_proj).astype(bf)
    g_proj = t_dot(act, cot)
    g_fc = t_dot(normed2, d_pre_b)
    g_bfc = jnp.sum(d_pre, axis=0)

    cot_f = cot_own.astype(f32)
    d_norm2, g_ln2g, g_ln2b = norm_back(hidden, ln2_gain, d_normed2)
    d_hidden = cot_f + d_norm2
    d_hidden_b = plane_gather(d_hidden.astype(bf))
    g_out = t_dot(attended, d_hidden_b)
    d_attended = dot_t(d_hidden_b, wout).astype(bf)
    d_query, d_key, d_value = attention_back(
        query, key, value, attended, d_attended, allowed, saved, heads
    )
    d_query_b, d_key_b, d_value_b = d_query.astype(bf), d_key.astype(bf), d_value.astype(bf)
    d_normed1 = plane_scatter(
        dot_t(d_query_b, wqkv[0]) + dot_t(d_key_b, wqkv[1]) + dot_t(d_value_b, wqkv[2])
    )
    g_qkv = jnp.stack([t_dot(normed1, d_query_b), t_dot(normed1, d_key_b), t_dot(normed1, d_value_b)])
    d_norm1, g_ln1g, g_ln1b = norm_back(x_f, ln1_gain, d_normed1)
    grad_inputs = (d_hidden + d_norm1).astype(bf)

    def home(values):
        return lax.all_gather(swap_planes(values, shards), "tp", axis=0, tiled=True)

    def owner(grad, split, concat):
        moved = all_to_all(grad.astype(bf), shards, split, concat)
        return lax.psum(moved, "ctx").astype(f32)

    sum_proj = owner(g_proj, 1, 0)
    sum_fc = owner(g_fc, 0, 1)
    sum_out = owner(g_out, 1, 0)
    sum_qkv = owner(g_qkv, 1, 2)
    col = t * b_qv.shape[1] + s * width
    g_bqv = jnp.stack([jnp.sum(d_query, axis=0), jnp.sum(d_value, axis=0)])
    full_bqv = lax.dynamic_update_slice(jnp.zeros((2, b_qv.shape[1] * cores), f32), g_bqv, (0, col))
    full_bfc = lax.dynamic_update_slice(
        jnp.zeros((b_fc.shape[0] * cores,), f32), g_bfc, (t * b_fc.shape[0] + s * units,)
    )
    packed = jnp.concatenate(
        [
            full_bqv.reshape(-1),
            full_bfc,
            jnp.sum(d_hidden, axis=0),
            jnp.sum(cot_f, axis=0),
            g_ln1g,
            g_ln1b,
            g_ln2g,
            g_ln2b,
        ]
    )
    packed = lax.psum(packed, ("shard", "ctx", "tp"))
    at = full_bqv.size
    sum_bqv = lax.dynamic_slice_in_dim(
        packed[:at].reshape(full_bqv.shape), t * b_qv.shape[1], b_qv.shape[1], axis=1
    )
    sum_bfc = lax.dynamic_slice_in_dim(packed, at + t * b_fc.shape[0], b_fc.shape[0])
    at = at + full_bfc.size
    rest = packed[at:].reshape(6, model)
    return (
        home(outputs),
        home(grad_inputs),
        sum_qkv,
        sum_out,
        sum_fc,
        sum_proj,
        sum_bqv,
        rest[0],
        sum_bfc,
        rest[1],
        rest[2],
        rest[3],
        rest[4],
        rest[5],
    )


def solution(mesh):
    in_specs = (
        P(("shard", "ctx"), None),
        P("shard", None),
        P(("shard", "ctx"), None),
        P(None, "shard", "tp"),
        P("tp", "shard"),
        P("shard", "tp"),
        P("tp", "shard"),
        P(None, "tp"),
        P(),
        P("tp"),
        P(),
        P(),
        P(),
        P(),
        P(),
    )
    out_specs = (
        P(("shard", "ctx"), None),
        P(("shard", "ctx"), None),
        P(None, "shard", "tp"),
        P("tp", "shard"),
        P("shard", "tp"),
        P("tp", "shard"),
        P(None, "tp"),
        P(),
        P("tp"),
        P(),
        P(),
        P(),
        P(),
        P(),
    )
    count = mesh.shape["shard"]
    square = count == mesh.shape["ctx"] and count & (count - 1) == 0
    body = on_device_plane if square else on_device_general
    return jax.shard_map(
        body, mesh=mesh, in_specs=in_specs, out_specs=out_specs, check_vma=False
    )
```

```python
import jax
import jax.numpy as jnp
from jax import lax
from jax.experimental import pallas as pl
from jax.experimental.pallas import tpu as pltpu
from jax.sharding import PartitionSpec as P

HEAD_DIM = 64


def layer_norm(values, gain, shift):
    mean = jnp.mean(values, axis=-1, keepdims=True)
    centred = values - mean
    spread = jnp.mean(centred * centred, axis=-1, keepdims=True)
    return centred * lax.rsqrt(spread + 1e-05) * gain + shift


def gelu_tanh(values):
    return (
        0.5
        * values
        * (1.0 + jnp.tanh(0.7978845608028654 * (values + 0.044715 * values * values * values)))
    )


def segment_ids(lengths, count):
    ends = jnp.cumsum(lengths)
    places = jnp.arange(count, dtype=jnp.int32)
    return jnp.sum((places[:, None] >= ends[None, :]).astype(jnp.int32), axis=1)


def dot32(left, right):
    return jnp.dot(left, right, preferred_element_type=jnp.float32)


def on_device_general(
    inputs,
    lengths,
    cotangent,
    w_qkv,
    w_out,
    w_fc,
    w_proj,
    b_qv,
    b_out,
    b_fc,
    b_proj,
    ln1_gain,
    ln1_bias,
    ln2_gain,
    ln2_bias,
):
    bf = jnp.bfloat16
    f32 = jnp.float32
    rows = inputs.shape[0]
    parts = lax.axis_size("ctx")
    block = rows * parts
    local_width = b_qv.shape[1]
    local_heads = local_width // HEAD_DIM
    seg_all = segment_ids(lengths[0], block)
    first = lax.axis_index("ctx") * rows
    q_pos = first + jnp.arange(rows, dtype=jnp.int32)
    q_seg = lax.dynamic_slice_in_dim(seg_all, first, rows)
    wq_all, wo_all, wfc_all, wproj_all = (
        lax.all_gather(w_qkv, "shard", axis=1, tiled=True),
        lax.all_gather(w_out, "shard", axis=1, tiled=True),
        lax.all_gather(w_fc, "shard", axis=0, tiled=True),
        lax.all_gather(w_proj, "shard", axis=1, tiled=True),
    )
    x_f = inputs.astype(f32)
    normed1 = layer_norm(x_f, ln1_gain, ln1_bias).astype(bf)
    query = ((dot32(normed1, wq_all[0]) + b_qv[0]) * 0.125).astype(bf)
    key = dot32(normed1, wq_all[1]).astype(bf)
    value = (dot32(normed1, wq_all[2]) + b_qv[1]).astype(bf)
    q3 = query.reshape(rows, local_heads, HEAD_DIM)

    def allowed_for(start, count):
        k_pos = start + jnp.arange(count, dtype=jnp.int32)
        k_seg = lax.dynamic_slice_in_dim(seg_all, start, count)
        return (k_pos[None, :] <= q_pos[:, None]) & (k_seg[None, :] == q_seg[:, None])

    k_piece = lax.all_gather(key, "ctx", axis=0, tiled=True)
    v_piece = lax.all_gather(value, "ctx", axis=0, tiled=True)
    count = k_piece.shape[0]
    allowed = allowed_for(jnp.int32(0), count)
    scores = jnp.einsum(
        "rhd,nhd->hrn",
        q3,
        k_piece.reshape(count, local_heads, HEAD_DIM),
        preferred_element_type=f32,
    )
    weights = jnp.where(allowed[None], jnp.exp(scores), 0.0)
    total = jnp.sum(weights, axis=2)
    acc = jnp.einsum(
        "hrn,nhd->hrd",
        weights.astype(bf),
        v_piece.reshape(count, local_heads, HEAD_DIM),
        preferred_element_type=f32,
    )
    total, acc = (total, acc)
    log_total = jnp.log(total)
    attended = (acc / total[:, :, None]).transpose(1, 0, 2).reshape(rows, local_width).astype(bf)
    mixed = lax.psum(dot32(attended, wo_all).astype(jnp.bfloat16), "tp").astype(jnp.float32)
    hidden = x_f + mixed + b_out
    normed2 = layer_norm(hidden, ln2_gain, ln2_bias).astype(bf)
    pre = dot32(normed2, wfc_all) + b_fc
    act = gelu_tanh(pre).astype(bf)
    mlp_total = lax.psum(dot32(act, wproj_all).astype(jnp.bfloat16), "tp").astype(jnp.float32)
    outputs = (hidden + mlp_total + b_proj).astype(bf)
    wq_back, wo_back, wfc_back, wproj_back = (
        lax.all_gather(w_qkv, "shard", axis=1, tiled=True),
        lax.all_gather(w_out, "shard", axis=1, tiled=True),
        lax.all_gather(w_fc, "shard", axis=0, tiled=True),
        lax.all_gather(w_proj, "shard", axis=1, tiled=True),
    )
    grad_f = cotangent.astype(f32)
    g_bproj = jnp.sum(grad_f, axis=0)
    g_proj = dot32(act.T, cotangent)
    d_act = dot32(cotangent, wproj_back.T)
    gelu_back = jax.vjp(gelu_tanh, pre)[1]
    d_pre = gelu_back(d_act)[0]
    g_bfc = jnp.sum(d_pre, axis=0)
    d_pre_b = d_pre.astype(bf)
    g_fc = dot32(normed2.T, d_pre_b)
    d_normed2 = lax.psum(dot32(d_pre_b, wfc_back.T).astype(jnp.bfloat16), "tp").astype(jnp.float32)
    norm_back2 = jax.vjp(layer_norm, hidden, ln2_gain, ln2_bias)[1]
    d_norm2, g_ln2g, g_ln2b = norm_back2(d_normed2)
    d_hidden = grad_f + d_norm2
    g_bout = jnp.sum(d_hidden, axis=0)
    d_hidden_b = d_hidden.astype(bf)
    g_out = dot32(attended.T, d_hidden_b)
    d_attended = dot32(d_hidden_b, wo_back.T).astype(bf)
    da3 = d_attended.reshape(rows, local_heads, HEAD_DIM)
    at3 = attended.reshape(rows, local_heads, HEAD_DIM)
    delta = jnp.einsum("rhd,rhd->hr", da3, at3, preferred_element_type=f32)
    key_all, value_all = (
        lax.all_gather(key, "ctx", axis=0, tiled=True),
        lax.all_gather(value, "ctx", axis=0, tiled=True),
    )
    key_blocks = key_all.reshape(parts, rows, local_heads, HEAD_DIM)
    value_blocks = value_all.reshape(parts, rows, local_heads, HEAD_DIM)
    starts = jnp.arange(parts, dtype=jnp.int32) * rows

    def back_piece(d_query_acc, inputs_piece):
        k_piece, v_piece, start = inputs_piece
        allowed = allowed_for(start, rows)
        scores = jnp.einsum("rhd,nhd->hrn", q3, k_piece, preferred_element_type=f32)
        probs = jnp.where(allowed[None], jnp.exp(scores - log_total[:, :, None]), 0.0)
        d_v = jnp.einsum("hrn,rhd->nhd", probs.astype(bf), da3, preferred_element_type=f32)
        d_probs = jnp.einsum("rhd,nhd->hrn", da3, v_piece, preferred_element_type=f32)
        d_scores_b = (probs * (d_probs - delta[:, :, None])).astype(bf)
        d_query_acc = d_query_acc + jnp.einsum(
            "hrn,nhd->rhd", d_scores_b, k_piece, preferred_element_type=f32
        )
        d_k = jnp.einsum("hrn,rhd->nhd", d_scores_b, q3, preferred_element_type=f32)
        return (d_query_acc, (d_k.reshape(rows, local_width), d_v.reshape(rows, local_width)))

    zero_query = jnp.zeros((rows, local_heads, HEAD_DIM), f32)
    d_query_acc, (d_key_terms, d_value_terms) = lax.scan(
        back_piece, zero_query, (key_blocks, value_blocks, starts)
    )
    d_key, d_value = (
        lax.psum_scatter(
            d_key_terms.reshape(block, local_width).astype(jnp.bfloat16),
            "ctx",
            scatter_dimension=0,
            tiled=True,
        ).astype(jnp.float32),
        lax.psum_scatter(
            d_value_terms.reshape(block, local_width).astype(jnp.bfloat16),
            "ctx",
            scatter_dimension=0,
            tiled=True,
        ).astype(jnp.float32),
    )
    d_query = d_query_acc.reshape(rows, local_width) * 0.125
    g_bqv = jnp.stack([jnp.sum(d_query, axis=0), jnp.sum(d_value, axis=0)])
    d_query_b = d_query.astype(bf)
    d_key_b = d_key.astype(bf)
    d_value_b = d_value.astype(bf)
    g_qkv = jnp.stack(
        [dot32(normed1.T, d_query_b), dot32(normed1.T, d_key_b), dot32(normed1.T, d_value_b)]
    )
    d_local = (
        dot32(d_query_b, wq_back[0].T)
        + dot32(d_key_b, wq_back[1].T)
        + dot32(d_value_b, wq_back[2].T)
    )
    d_normed1 = lax.psum(d_local.astype(jnp.bfloat16), "tp").astype(jnp.float32)
    norm_back1 = jax.vjp(layer_norm, x_f, ln1_gain, ln1_bias)[1]
    d_norm1, g_ln1g, g_ln1b = norm_back1(d_normed1)
    grad_inputs = (d_hidden + d_norm1).astype(bf)
    part_qkv, part_out, part_fc, part_proj = (
        lax.psum_scatter(
            g_qkv.astype(jnp.bfloat16), "shard", scatter_dimension=1, tiled=True
        ).astype(jnp.float32),
        lax.psum_scatter(
            g_out.astype(jnp.bfloat16), "shard", scatter_dimension=1, tiled=True
        ).astype(jnp.float32),
        lax.psum_scatter(
            g_fc.astype(jnp.bfloat16), "shard", scatter_dimension=0, tiled=True
        ).astype(jnp.float32),
        lax.psum_scatter(
            g_proj.astype(jnp.bfloat16), "shard", scatter_dimension=1, tiled=True
        ).astype(jnp.float32),
    )
    sum_qkv, sum_out, sum_fc, sum_proj = (
        lax.psum(part_qkv.astype(jnp.bfloat16), "ctx").astype(jnp.float32),
        lax.psum(part_out.astype(jnp.bfloat16), "ctx").astype(jnp.float32),
        lax.psum(part_fc.astype(jnp.bfloat16), "ctx").astype(jnp.float32),
        lax.psum(part_proj.astype(jnp.bfloat16), "ctx").astype(jnp.float32),
    )
    small = lax.psum(
        (g_bqv, g_bout, g_bfc, g_bproj, g_ln1g, g_ln1b, g_ln2g, g_ln2b), ("shard", "ctx")
    )
    return (
        outputs,
        grad_inputs,
        sum_qkv,
        sum_out,
        sum_fc,
        sum_proj,
        small[0],
        small[1],
        small[2],
        small[3],
        small[4],
        small[5],
        small[6],
        small[7],
    )


MESH = pl.DeviceIdType.MESH
VMEM = pl.BlockSpec(memory_space=pltpu.VMEM)


def greet(peers):
    barrier = pltpu.get_barrier_semaphore()
    for peer in peers:
        pl.semaphore_signal(barrier, inc=1, device_id=peer, device_id_type=MESH)
    pl.semaphore_wait(barrier, len(peers))


def send(src, dst, send_sem, recv_sem, peer):
    copy = pltpu.make_async_remote_copy(
        src_ref=src,
        dst_ref=dst,
        send_sem=send_sem,
        recv_sem=recv_sem,
        device_id=peer,
        device_id_type=MESH,
    )
    copy.start()
    return copy


def comm_call(kernel, out_shape, scratch, ident, cost, *operands):
    many = isinstance(out_shape, (list, tuple))
    return pl.pallas_call(
        kernel,
        out_shape=out_shape,
        in_specs=[VMEM] * len(operands),
        out_specs=[VMEM] * len(out_shape) if many else VMEM,
        scratch_shapes=scratch,
        compiler_params=pltpu.CompilerParams(collective_id=ident, has_side_effects=True),
        cost_estimate=pl.CostEstimate(flops=0, bytes_accessed=cost, transcendentals=0),
    )(*operands)


def all_to_all(arrays, cuts, ident):
    count = lax.axis_size("shard")
    shapes = []
    for array, (split, concat) in zip(arrays, cuts):
        shape = list(array.shape)
        shape[split] //= count
        shape[concat] *= count
        shapes.append(jax.ShapeDtypeStruct(tuple(shape), array.dtype))
    total = len(arrays)

    def kernel(*refs):
        ins, outs = refs[:total], refs[total : 2 * total]
        send_sem, recv_sem, own_sem = refs[2 * total :]
        me = lax.axis_index("shard")
        greet([{"shard": me ^ step} for step in range(1, count)])

        def view(ref, axis, index, size):
            start = pl.multiple_of(index * size, size)
            return ref.at[tuple(pl.ds(start, size) if d == axis else slice(None) for d in range(len(ref.shape)))]

        copies = []
        for a, (split, concat) in enumerate(cuts):
            width = ins[a].shape[split] // count
            depth = ins[a].shape[concat]
            for step in range(count - 1, 0, -1):
                at = a * (count - 1) + step - 1
                copies.append(
                    send(
                        view(ins[a], split, me ^ step, width),
                        view(outs[a], concat, me, depth),
                        send_sem.at[at],
                        recv_sem.at[at],
                        {"shard": me ^ step},
                    )
                )
            own = pltpu.make_async_copy(
                view(ins[a], split, me, width), view(outs[a], concat, me, depth), own_sem.at[a]
            )
            own.start()
            copies.append(own)
        for copy in copies:
            copy.wait()

    sems = total * (count - 1)
    return comm_call(
        kernel,
        shapes,
        [
            pltpu.SemaphoreType.DMA((sems,)),
            pltpu.SemaphoreType.DMA((sems,)),
            pltpu.SemaphoreType.DMA((total,)),
        ],
        ident,
        1 << 24,
        *arrays,
    )


def plane_gather(values):
    count = lax.axis_size("shard")
    rows, cols = values.shape

    def kernel(x_ref, o_ref, send_sem, recv_sem, pass_sem, pair_sem, own_sem):
        s, t = lax.axis_index("shard"), lax.axis_index("tp")
        other = {"tp": 1 - t}
        greet([other] + [{"shard": s ^ step} for step in range(1, count)])

        def slot(index):
            return o_ref.at[pl.ds(pl.multiple_of((index * 2 + t) * rows, rows), rows)]

        own = pltpu.make_async_copy(x_ref, slot(s), own_sem)
        own.start()
        copies = {}
        for step in range(count - 1, 0, -1):
            copies[step] = send(
                x_ref, slot(s), send_sem.at[step - 1], recv_sem.at[step - 1], {"shard": s ^ step}
            )
        passed = [send(x_ref, slot(s), pass_sem.at[0], pair_sem.at[0], other)]
        for step in range(1, count):
            copies[step].wait_recv()
            passed.append(
                send(slot(s ^ step), slot(s ^ step), pass_sem.at[step], pair_sem.at[step], other)
            )
        for copy in passed:
            copy.wait()
        for step in range(1, count):
            copies[step].wait_send()
        own.wait()

    return comm_call(
        kernel,
        jax.ShapeDtypeStruct((rows * count * 2, cols), values.dtype),
        [
            pltpu.SemaphoreType.DMA((count - 1,)),
            pltpu.SemaphoreType.DMA((count - 1,)),
            pltpu.SemaphoreType.DMA((count,)),
            pltpu.SemaphoreType.DMA((count,)),
            pltpu.SemaphoreType.DMA,
        ],
        1,
        1 << 24,
        values,
    )


def plane_scatter(values):
    count = lax.axis_size("shard")
    rows, cols = values.shape[0] // (count * 2), values.shape[1]
    f32 = jnp.float32
    bf = jnp.bfloat16

    def kernel(p_ref, o_ref, got, staged, arrived, pass_sem, pair_sem, send_sem, recv_sem):
        s, t = lax.axis_index("shard"), lax.axis_index("tp")
        other = {"tp": 1 - t}
        greet([other] + [{"shard": s ^ step} for step in range(1, count)])

        def chunk(index, core):
            return p_ref.at[pl.ds(pl.multiple_of((index * 2 + core) * rows, rows), rows)]

        order = list(range(count - 1, -1, -1))
        first = {}
        for step in order:
            first[step] = send(
                chunk(s ^ step, 1 - t), got.at[step], pass_sem.at[step], pair_sem.at[step], other
            )
        second = []
        for step in order:
            first[step].wait_recv()
            total = chunk(s ^ step, t)[...].astype(f32) + got[step].astype(f32)
            if step > 0:
                staged[step - 1] = total.astype(bf)
                second.append(
                    send(
                        staged.at[step - 1],
                        arrived.at[step - 1],
                        send_sem.at[step - 1],
                        recv_sem.at[step - 1],
                        {"shard": s ^ step},
                    )
                )
            else:
                o_ref[...] = total
        for copy, step in zip(second, order):
            copy.wait_recv()
            o_ref[...] += arrived[step - 1].astype(f32)
        for step in order:
            first[step].wait_send()
        for copy in second:
            copy.wait_send()

    return comm_call(
        kernel,
        jax.ShapeDtypeStruct((rows, cols), f32),
        [
            pltpu.VMEM((count, rows, cols), bf),
            pltpu.VMEM((count - 1, rows, cols), bf),
            pltpu.VMEM((count - 1, rows, cols), bf),
            pltpu.SemaphoreType.DMA((count,)),
            pltpu.SemaphoreType.DMA((count,)),
            pltpu.SemaphoreType.DMA((count - 1,)),
            pltpu.SemaphoreType.DMA((count - 1,)),
        ],
        2,
        1 << 24,
        values.astype(bf),
    )


def sum_everywhere(values):
    shards, lines = lax.axis_size("shard"), lax.axis_size("ctx")
    shape = values.shape

    def kernel(x_ref, o_ref, got, staged, arrived, send_sem, recv_sem, line_send, line_recv):
        s, c, t = lax.axis_index("shard"), lax.axis_index("ctx"), lax.axis_index("tp")
        plane = [
            {"shard": s ^ step, "tp": 1 - t if swap else t}
            for step in range(shards)
            for swap in range(2)
            if step or swap
        ]
        line = [{"ctx": c ^ step} for step in range(1, lines)]
        greet(plane + line)
        copies = [
            send(x_ref, got.at[i], send_sem.at[i], recv_sem.at[i], peer)
            for i, peer in enumerate(plane)
        ]
        total = x_ref[...]
        for i, copy in enumerate(copies):
            copy.wait_recv()
            total = total + got[i]
        staged[...] = total
        o_ref[...] = total
        lines_out = [
            send(staged, arrived.at[i], line_send.at[i], line_recv.at[i], peer)
            for i, peer in enumerate(line)
        ]
        for i, copy in enumerate(lines_out):
            copy.wait_recv()
            o_ref[...] += arrived[i]
        for copy in copies + lines_out:
            copy.wait_send()

    near, far = shards * 2 - 1, lines - 1
    return comm_call(
        kernel,
        jax.ShapeDtypeStruct(shape, values.dtype),
        [
            pltpu.VMEM((near,) + shape, values.dtype),
            pltpu.VMEM(shape, values.dtype),
            pltpu.VMEM((far,) + shape, values.dtype),
            pltpu.SemaphoreType.DMA((near,)),
            pltpu.SemaphoreType.DMA((near,)),
            pltpu.SemaphoreType.DMA((far,)),
            pltpu.SemaphoreType.DMA((far,)),
        ],
        3,
        1 << 22,
        values,
    )


def swap_planes(values, count):
    pairs = [(a * count + b, b * count + a) for a in range(count) for b in range(count)]
    return lax.ppermute(values, ("shard", "ctx"), pairs)


def norm_back(values, gain, d_out):
    mean = jnp.mean(values, axis=-1, keepdims=True)
    centred = values - mean
    scale = lax.rsqrt(jnp.mean(centred * centred, axis=-1, keepdims=True) + 1e-05)
    unit = centred * scale
    d_unit = d_out * gain
    first = jnp.mean(d_unit, axis=-1, keepdims=True)
    second = jnp.mean(d_unit * unit, axis=-1, keepdims=True)
    d_values = (d_unit - first - unit * second) * scale
    return d_values, jnp.sum(d_out * unit, axis=0), jnp.sum(d_out, axis=0)


def attention(query, key, value, allowed, heads):
    f32 = jnp.float32
    parts = []
    saved = []
    for head in range(heads):
        cols = slice(head * HEAD_DIM, (head + 1) * HEAD_DIM)
        scores = lax.dot_general(
            query[:, cols], key[:, cols], (((1,), (1,)), ((), ())), preferred_element_type=f32
        )
        weights = jnp.where(allowed, jnp.exp(scores), 0.0)
        total = jnp.sum(weights, axis=1, keepdims=True)
        parts.append(dot32(weights.astype(jnp.bfloat16), value[:, cols]) / total)
        saved.append(jnp.log(total))
    return jnp.concatenate(parts, axis=1).astype(jnp.bfloat16), saved


def attention_back(query, key, value, attended, d_attended, allowed, saved, heads):
    f32 = jnp.float32
    bf = jnp.bfloat16
    d_q, d_k, d_v = [], [], []
    for head in range(heads):
        cols = slice(head * HEAD_DIM, (head + 1) * HEAD_DIM)
        q, k, v, da = query[:, cols], key[:, cols], value[:, cols], d_attended[:, cols]
        delta = jnp.sum(da.astype(f32) * attended[:, cols].astype(f32), axis=1, keepdims=True)
        scores = lax.dot_general(q, k, (((1,), (1,)), ((), ())), preferred_element_type=f32)
        probs = jnp.where(allowed, jnp.exp(scores - saved[head]), 0.0)
        d_v.append(
            lax.dot_general(
                probs.astype(bf), da, (((0,), (0,)), ((), ())), preferred_element_type=f32
            )
        )
        d_probs = lax.dot_general(da, v, (((1,), (1,)), ((), ())), preferred_element_type=f32)
        d_scores = (probs * (d_probs - delta)).astype(bf)
        d_q.append(dot32(d_scores, k))
        d_k.append(
            lax.dot_general(d_scores, q, (((0,), (0,)), ((), ())), preferred_element_type=f32)
        )
    join = lambda items: jnp.concatenate(items, axis=1)
    return join(d_q) * 0.125, join(d_k), join(d_v)


def t_dot(left, right):
    return lax.dot_general(left, right, (((0,), (0,)), ((), ())), preferred_element_type=jnp.float32)


def dot_t(left, right):
    return lax.dot_general(left, right, (((1,), (1,)), ((), ())), preferred_element_type=jnp.float32)


def on_device_plane(
    inputs,
    lengths,
    cotangent,
    w_qkv,
    w_out,
    w_fc,
    w_proj,
    b_qv,
    b_out,
    b_fc,
    b_proj,
    ln1_gain,
    ln1_bias,
    ln2_gain,
    ln2_bias,
):
    bf = jnp.bfloat16
    f32 = jnp.float32
    shards = lax.axis_size("shard")
    cores = lax.axis_size("tp")
    s = lax.axis_index("shard")
    t = lax.axis_index("tp")
    rows = inputs.shape[0] // cores
    block = rows * cores * shards
    model = inputs.shape[1]
    width = b_qv.shape[1] // shards
    heads = width // HEAD_DIM
    units = b_fc.shape[0] // shards
    mine = lambda array: lax.dynamic_slice_in_dim(array, t * rows, rows, axis=0)

    x_f = swap_planes(mine(inputs), shards).astype(f32)
    lens = swap_planes(lengths, shards)[0]
    cot_own = swap_planes(mine(cotangent), shards)
    normed1 = plane_gather(layer_norm(x_f, ln1_gain, ln1_bias).astype(bf))
    wqkv, wout, wfc, wproj = all_to_all(
        [w_qkv, w_out, w_fc, w_proj], [(2, 1), (0, 1), (1, 0), (0, 1)], 4
    )
    cot = plane_gather(cot_own)
    b_qv_own = lax.dynamic_slice_in_dim(b_qv, s * width, width, axis=1)
    b_fc_own = lax.dynamic_slice_in_dim(b_fc, s * units, units, axis=0)

    seg = segment_ids(lens, block)
    places = jnp.arange(block, dtype=jnp.int32)
    allowed = (places[None, :] <= places[:, None]) & (seg[None, :] == seg[:, None])

    query = ((dot32(normed1, wqkv[0]) + b_qv_own[0]) * 0.125).astype(bf)
    key = dot32(normed1, wqkv[1]).astype(bf)
    value = (dot32(normed1, wqkv[2]) + b_qv_own[1]).astype(bf)
    attended, saved = attention(query, key, value, allowed, heads)
    hidden = x_f + plane_scatter(dot32(attended, wout)) + b_out
    normed2 = plane_gather(layer_norm(hidden, ln2_gain, ln2_bias).astype(bf))
    pre = dot32(normed2, wfc) + b_fc_own
    act = gelu_tanh(pre).astype(bf)
    d_act = dot_t(cot, wproj)
    d_pre = jax.vjp(gelu_tanh, pre)[1](d_act)[0]
    d_pre_b = d_pre.astype(bf)
    d_normed2 = plane_scatter(dot_t(d_pre_b, wfc))
    mlp_total = plane_scatter(dot32(act, wproj))
    outputs = (hidden + mlp_total + b_proj).astype(bf)
    g_proj = t_dot(act, cot)
    g_fc = t_dot(normed2, d_pre_b)
    g_bfc = jnp.sum(d_pre, axis=0)

    cot_f = cot_own.astype(f32)
    d_norm2, g_ln2g, g_ln2b = norm_back(hidden, ln2_gain, d_normed2)
    d_hidden = cot_f + d_norm2
    d_hidden_b = plane_gather(d_hidden.astype(bf))
    g_out = t_dot(attended, d_hidden_b)
    d_attended = dot_t(d_hidden_b, wout).astype(bf)
    d_query, d_key, d_value = attention_back(
        query, key, value, attended, d_attended, allowed, saved, heads
    )
    d_query_b, d_key_b, d_value_b = d_query.astype(bf), d_key.astype(bf), d_value.astype(bf)
    d_normed1 = plane_scatter(
        dot_t(d_query_b, wqkv[0]) + dot_t(d_key_b, wqkv[1]) + dot_t(d_value_b, wqkv[2])
    )
    g_qkv = jnp.stack([t_dot(normed1, d_query_b), t_dot(normed1, d_key_b), t_dot(normed1, d_value_b)])
    d_norm1, g_ln1g, g_ln1b = norm_back(x_f, ln1_gain, d_normed1)
    grad_inputs = (d_hidden + d_norm1).astype(bf)

    def home(values):
        return lax.all_gather(swap_planes(values, shards), "tp", axis=0, tiled=True)

    early = all_to_all([g_proj.astype(bf), g_fc.astype(bf)], [(1, 0), (0, 1)], 5)

    def line_sum(values):
        part = lax.psum_scatter(values, "ctx", scatter_dimension=0, tiled=True)
        return lax.all_gather(part, "ctx", axis=0, tiled=True).astype(f32)

    sum_proj, sum_fc = line_sum(early[0]), line_sum(early[1])
    late = all_to_all([g_out.astype(bf), g_qkv.astype(bf)], [(1, 0), (1, 2)], 6)
    sum_out = lax.psum(late[0], "ctx").astype(f32)
    sum_qkv = lax.psum(late[1], "ctx").astype(f32)
    col = t * b_qv.shape[1] + s * width
    g_bqv = jnp.stack([jnp.sum(d_query, axis=0), jnp.sum(d_value, axis=0)])
    full_bqv = lax.dynamic_update_slice(jnp.zeros((2, b_qv.shape[1] * cores), f32), g_bqv, (0, col))
    full_bfc = lax.dynamic_update_slice(
        jnp.zeros((b_fc.shape[0] * cores,), f32), g_bfc, (t * b_fc.shape[0] + s * units,)
    )
    packed = jnp.concatenate(
        [
            full_bqv.reshape(-1),
            full_bfc,
            jnp.sum(d_hidden, axis=0),
            jnp.sum(cot_f, axis=0),
            g_ln1g,
            g_ln1b,
            g_ln2g,
            g_ln2b,
        ]
    )
    packed = sum_everywhere(packed.reshape(-1, 128)).reshape(-1)
    at = full_bqv.size
    sum_bqv = lax.dynamic_slice_in_dim(
        packed[:at].reshape(full_bqv.shape), t * b_qv.shape[1], b_qv.shape[1], axis=1
    )
    sum_bfc = lax.dynamic_slice_in_dim(packed, at + t * b_fc.shape[0], b_fc.shape[0])
    at = at + full_bfc.size
    rest = packed[at:].reshape(6, model)
    return (
        home(outputs),
        home(grad_inputs),
        sum_qkv,
        sum_out,
        sum_fc,
        sum_proj,
        sum_bqv,
        rest[0],
        sum_bfc,
        rest[1],
        rest[2],
        rest[3],
        rest[4],
        rest[5],
    )


def solution(mesh):
    in_specs = (
        P(("shard", "ctx"), None),
        P("shard", None),
        P(("shard", "ctx"), None),
        P(None, "shard", "tp"),
        P("tp", "shard"),
        P("shard", "tp"),
        P("tp", "shard"),
        P(None, "tp"),
        P(),
        P("tp"),
        P(),
        P(),
        P(),
        P(),
        P(),
    )
    out_specs = (
        P(("shard", "ctx"), None),
        P(("shard", "ctx"), None),
        P(None, "shard", "tp"),
        P("tp", "shard"),
        P("shard", "tp"),
        P("tp", "shard"),
        P(None, "tp"),
        P(),
        P("tp"),
        P(),
        P(),
        P(),
        P(),
        P(),
    )
    count = mesh.shape["shard"]
    square = count == mesh.shape["ctx"] and count & (count - 1) == 0 and mesh.shape["tp"] == 2
    body = on_device_plane if square else on_device_general
    return jax.shard_map(
        body, mesh=mesh, in_specs=in_specs, out_specs=out_specs, check_vma=False
    )
```

```python
import jax
import jax.numpy as jnp
from jax import lax
from jax.experimental import pallas as pl
from jax.experimental.pallas import tpu as pltpu
from jax.sharding import PartitionSpec as P

HEAD_DIM = 64


def layer_norm(values, gain, shift):
    mean = jnp.mean(values, axis=-1, keepdims=True)
    centred = values - mean
    spread = jnp.mean(centred * centred, axis=-1, keepdims=True)
    return centred * lax.rsqrt(spread + 1e-05) * gain + shift


def gelu_tanh(values):
    return (
        0.5
        * values
        * (1.0 + jnp.tanh(0.7978845608028654 * (values + 0.044715 * values * values * values)))
    )


def segment_ids(lengths, count):
    ends = jnp.cumsum(lengths)
    places = jnp.arange(count, dtype=jnp.int32)
    return jnp.sum((places[:, None] >= ends[None, :]).astype(jnp.int32), axis=1)


def dot32(left, right):
    return jnp.dot(left, right, preferred_element_type=jnp.float32)


def on_device_general(
    inputs,
    lengths,
    cotangent,
    w_qkv,
    w_out,
    w_fc,
    w_proj,
    b_qv,
    b_out,
    b_fc,
    b_proj,
    ln1_gain,
    ln1_bias,
    ln2_gain,
    ln2_bias,
):
    bf = jnp.bfloat16
    f32 = jnp.float32
    rows = inputs.shape[0]
    parts = lax.axis_size("ctx")
    block = rows * parts
    local_width = b_qv.shape[1]
    local_heads = local_width // HEAD_DIM
    seg_all = segment_ids(lengths[0], block)
    first = lax.axis_index("ctx") * rows
    q_pos = first + jnp.arange(rows, dtype=jnp.int32)
    q_seg = lax.dynamic_slice_in_dim(seg_all, first, rows)
    wq_all, wo_all, wfc_all, wproj_all = (
        lax.all_gather(w_qkv, "shard", axis=1, tiled=True),
        lax.all_gather(w_out, "shard", axis=1, tiled=True),
        lax.all_gather(w_fc, "shard", axis=0, tiled=True),
        lax.all_gather(w_proj, "shard", axis=1, tiled=True),
    )
    x_f = inputs.astype(f32)
    normed1 = layer_norm(x_f, ln1_gain, ln1_bias).astype(bf)
    query = ((dot32(normed1, wq_all[0]) + b_qv[0]) * 0.125).astype(bf)
    key = dot32(normed1, wq_all[1]).astype(bf)
    value = (dot32(normed1, wq_all[2]) + b_qv[1]).astype(bf)
    q3 = query.reshape(rows, local_heads, HEAD_DIM)

    def allowed_for(start, count):
        k_pos = start + jnp.arange(count, dtype=jnp.int32)
        k_seg = lax.dynamic_slice_in_dim(seg_all, start, count)
        return (k_pos[None, :] <= q_pos[:, None]) & (k_seg[None, :] == q_seg[:, None])

    k_piece = lax.all_gather(key, "ctx", axis=0, tiled=True)
    v_piece = lax.all_gather(value, "ctx", axis=0, tiled=True)
    count = k_piece.shape[0]
    allowed = allowed_for(jnp.int32(0), count)
    scores = jnp.einsum(
        "rhd,nhd->hrn",
        q3,
        k_piece.reshape(count, local_heads, HEAD_DIM),
        preferred_element_type=f32,
    )
    weights = jnp.where(allowed[None], jnp.exp(scores), 0.0)
    total = jnp.sum(weights, axis=2)
    acc = jnp.einsum(
        "hrn,nhd->hrd",
        weights.astype(bf),
        v_piece.reshape(count, local_heads, HEAD_DIM),
        preferred_element_type=f32,
    )
    total, acc = (total, acc)
    log_total = jnp.log(total)
    attended = (acc / total[:, :, None]).transpose(1, 0, 2).reshape(rows, local_width).astype(bf)
    mixed = lax.psum(dot32(attended, wo_all).astype(jnp.bfloat16), "tp").astype(jnp.float32)
    hidden = x_f + mixed + b_out
    normed2 = layer_norm(hidden, ln2_gain, ln2_bias).astype(bf)
    pre = dot32(normed2, wfc_all) + b_fc
    act = gelu_tanh(pre).astype(bf)
    mlp_total = lax.psum(dot32(act, wproj_all).astype(jnp.bfloat16), "tp").astype(jnp.float32)
    outputs = (hidden + mlp_total + b_proj).astype(bf)
    wq_back, wo_back, wfc_back, wproj_back = (
        lax.all_gather(w_qkv, "shard", axis=1, tiled=True),
        lax.all_gather(w_out, "shard", axis=1, tiled=True),
        lax.all_gather(w_fc, "shard", axis=0, tiled=True),
        lax.all_gather(w_proj, "shard", axis=1, tiled=True),
    )
    grad_f = cotangent.astype(f32)
    g_bproj = jnp.sum(grad_f, axis=0)
    g_proj = dot32(act.T, cotangent)
    d_act = dot32(cotangent, wproj_back.T)
    gelu_back = jax.vjp(gelu_tanh, pre)[1]
    d_pre = gelu_back(d_act)[0]
    g_bfc = jnp.sum(d_pre, axis=0)
    d_pre_b = d_pre.astype(bf)
    g_fc = dot32(normed2.T, d_pre_b)
    d_normed2 = lax.psum(dot32(d_pre_b, wfc_back.T).astype(jnp.bfloat16), "tp").astype(jnp.float32)
    norm_back2 = jax.vjp(layer_norm, hidden, ln2_gain, ln2_bias)[1]
    d_norm2, g_ln2g, g_ln2b = norm_back2(d_normed2)
    d_hidden = grad_f + d_norm2
    g_bout = jnp.sum(d_hidden, axis=0)
    d_hidden_b = d_hidden.astype(bf)
    g_out = dot32(attended.T, d_hidden_b)
    d_attended = dot32(d_hidden_b, wo_back.T).astype(bf)
    da3 = d_attended.reshape(rows, local_heads, HEAD_DIM)
    at3 = attended.reshape(rows, local_heads, HEAD_DIM)
    delta = jnp.einsum("rhd,rhd->hr", da3, at3, preferred_element_type=f32)
    key_all, value_all = (
        lax.all_gather(key, "ctx", axis=0, tiled=True),
        lax.all_gather(value, "ctx", axis=0, tiled=True),
    )
    key_blocks = key_all.reshape(parts, rows, local_heads, HEAD_DIM)
    value_blocks = value_all.reshape(parts, rows, local_heads, HEAD_DIM)
    starts = jnp.arange(parts, dtype=jnp.int32) * rows

    def back_piece(d_query_acc, inputs_piece):
        k_piece, v_piece, start = inputs_piece
        allowed = allowed_for(start, rows)
        scores = jnp.einsum("rhd,nhd->hrn", q3, k_piece, preferred_element_type=f32)
        probs = jnp.where(allowed[None], jnp.exp(scores - log_total[:, :, None]), 0.0)
        d_v = jnp.einsum("hrn,rhd->nhd", probs.astype(bf), da3, preferred_element_type=f32)
        d_probs = jnp.einsum("rhd,nhd->hrn", da3, v_piece, preferred_element_type=f32)
        d_scores_b = (probs * (d_probs - delta[:, :, None])).astype(bf)
        d_query_acc = d_query_acc + jnp.einsum(
            "hrn,nhd->rhd", d_scores_b, k_piece, preferred_element_type=f32
        )
        d_k = jnp.einsum("hrn,rhd->nhd", d_scores_b, q3, preferred_element_type=f32)
        return (d_query_acc, (d_k.reshape(rows, local_width), d_v.reshape(rows, local_width)))

    zero_query = jnp.zeros((rows, local_heads, HEAD_DIM), f32)
    d_query_acc, (d_key_terms, d_value_terms) = lax.scan(
        back_piece, zero_query, (key_blocks, value_blocks, starts)
    )
    d_key, d_value = (
        lax.psum_scatter(
            d_key_terms.reshape(block, local_width).astype(jnp.bfloat16),
            "ctx",
            scatter_dimension=0,
            tiled=True,
        ).astype(jnp.float32),
        lax.psum_scatter(
            d_value_terms.reshape(block, local_width).astype(jnp.bfloat16),
            "ctx",
            scatter_dimension=0,
            tiled=True,
        ).astype(jnp.float32),
    )
    d_query = d_query_acc.reshape(rows, local_width) * 0.125
    g_bqv = jnp.stack([jnp.sum(d_query, axis=0), jnp.sum(d_value, axis=0)])
    d_query_b = d_query.astype(bf)
    d_key_b = d_key.astype(bf)
    d_value_b = d_value.astype(bf)
    g_qkv = jnp.stack(
        [dot32(normed1.T, d_query_b), dot32(normed1.T, d_key_b), dot32(normed1.T, d_value_b)]
    )
    d_local = (
        dot32(d_query_b, wq_back[0].T)
        + dot32(d_key_b, wq_back[1].T)
        + dot32(d_value_b, wq_back[2].T)
    )
    d_normed1 = lax.psum(d_local.astype(jnp.bfloat16), "tp").astype(jnp.float32)
    norm_back1 = jax.vjp(layer_norm, x_f, ln1_gain, ln1_bias)[1]
    d_norm1, g_ln1g, g_ln1b = norm_back1(d_normed1)
    grad_inputs = (d_hidden + d_norm1).astype(bf)
    part_qkv, part_out, part_fc, part_proj = (
        lax.psum_scatter(
            g_qkv.astype(jnp.bfloat16), "shard", scatter_dimension=1, tiled=True
        ).astype(jnp.float32),
        lax.psum_scatter(
            g_out.astype(jnp.bfloat16), "shard", scatter_dimension=1, tiled=True
        ).astype(jnp.float32),
        lax.psum_scatter(
            g_fc.astype(jnp.bfloat16), "shard", scatter_dimension=0, tiled=True
        ).astype(jnp.float32),
        lax.psum_scatter(
            g_proj.astype(jnp.bfloat16), "shard", scatter_dimension=1, tiled=True
        ).astype(jnp.float32),
    )
    sum_qkv, sum_out, sum_fc, sum_proj = (
        lax.psum(part_qkv.astype(jnp.bfloat16), "ctx").astype(jnp.float32),
        lax.psum(part_out.astype(jnp.bfloat16), "ctx").astype(jnp.float32),
        lax.psum(part_fc.astype(jnp.bfloat16), "ctx").astype(jnp.float32),
        lax.psum(part_proj.astype(jnp.bfloat16), "ctx").astype(jnp.float32),
    )
    small = lax.psum(
        (g_bqv, g_bout, g_bfc, g_bproj, g_ln1g, g_ln1b, g_ln2g, g_ln2b), ("shard", "ctx")
    )
    return (
        outputs,
        grad_inputs,
        sum_qkv,
        sum_out,
        sum_fc,
        sum_proj,
        small[0],
        small[1],
        small[2],
        small[3],
        small[4],
        small[5],
        small[6],
        small[7],
    )


MESH = pl.DeviceIdType.MESH
VMEM = pl.BlockSpec(memory_space=pltpu.VMEM)


def greet(peers):
    barrier = pltpu.get_barrier_semaphore()
    for peer in peers:
        pl.semaphore_signal(barrier, inc=1, device_id=peer, device_id_type=MESH)
    pl.semaphore_wait(barrier, len(peers))


def send(src, dst, send_sem, recv_sem, peer):
    copy = pltpu.make_async_remote_copy(
        src_ref=src,
        dst_ref=dst,
        send_sem=send_sem,
        recv_sem=recv_sem,
        device_id=peer,
        device_id_type=MESH,
    )
    copy.start()
    return copy


def comm_call(kernel, out_shape, scratch, ident, cost, *operands, after=()):
    many = isinstance(out_shape, (list, tuple))
    used, unread = len(operands), len(after)

    def body(*refs):
        kernel(*refs[:used], *refs[used + unread :])

    return pl.pallas_call(
        body,
        out_shape=out_shape,
        in_specs=[VMEM] * used + [pl.BlockSpec(memory_space=pl.ANY)] * unread,
        out_specs=[VMEM] * len(out_shape) if many else VMEM,
        scratch_shapes=scratch,
        compiler_params=pltpu.CompilerParams(collective_id=ident, has_side_effects=True),
        cost_estimate=pl.CostEstimate(flops=0, bytes_accessed=cost, transcendentals=0),
    )(*operands, *after)


def all_to_all(arrays, cuts, ident, after=()):
    count = lax.axis_size("shard")
    shapes = []
    for array, (split, concat) in zip(arrays, cuts):
        shape = list(array.shape)
        shape[split] //= count
        shape[concat] *= count
        shapes.append(jax.ShapeDtypeStruct(tuple(shape), array.dtype))
    total = len(arrays)

    def kernel(*refs):
        ins, outs = refs[:total], refs[total : 2 * total]
        send_sem, recv_sem, own_sem = refs[2 * total :]
        me = lax.axis_index("shard")
        greet([{"shard": me ^ step} for step in range(1, count)])

        def view(ref, axis, index, size):
            start = pl.multiple_of(index * size, size)
            return ref.at[tuple(pl.ds(start, size) if d == axis else slice(None) for d in range(len(ref.shape)))]

        copies = []
        for a, (split, concat) in enumerate(cuts):
            width = ins[a].shape[split] // count
            depth = ins[a].shape[concat]
            for step in range(count - 1, 0, -1):
                at = a * (count - 1) + step - 1
                copies.append(
                    send(
                        view(ins[a], split, me ^ step, width),
                        view(outs[a], concat, me, depth),
                        send_sem.at[at],
                        recv_sem.at[at],
                        {"shard": me ^ step},
                    )
                )
            own = pltpu.make_async_copy(
                view(ins[a], split, me, width), view(outs[a], concat, me, depth), own_sem.at[a]
            )
            own.start()
            copies.append(own)
        for copy in copies:
            copy.wait()

    sems = total * (count - 1)
    return comm_call(
        kernel,
        shapes,
        [
            pltpu.SemaphoreType.DMA((sems,)),
            pltpu.SemaphoreType.DMA((sems,)),
            pltpu.SemaphoreType.DMA((total,)),
        ],
        ident,
        1 << 24,
        *arrays,
        after=after,
    )


def hold(values, after):
    def kernel(x_ref, _, o_ref):
        o_ref[...] = x_ref[...]

    return pl.pallas_call(
        kernel,
        out_shape=jax.ShapeDtypeStruct(values.shape, values.dtype),
        in_specs=[VMEM, pl.BlockSpec(memory_space=pl.ANY)],
        out_specs=VMEM,
    )(values, after)


def plane_gather(values):
    count = lax.axis_size("shard")
    rows, cols = values.shape

    def kernel(x_ref, o_ref, send_sem, recv_sem, pass_sem, pair_sem, own_sem):
        s, t = lax.axis_index("shard"), lax.axis_index("tp")
        other = {"tp": 1 - t}
        greet([other] + [{"shard": s ^ step} for step in range(1, count)])

        def slot(index):
            return o_ref.at[pl.ds(pl.multiple_of((index * 2 + t) * rows, rows), rows)]

        own = pltpu.make_async_copy(x_ref, slot(s), own_sem)
        own.start()
        copies = {}
        for step in range(count - 1, 0, -1):
            copies[step] = send(
                x_ref, slot(s), send_sem.at[step - 1], recv_sem.at[step - 1], {"shard": s ^ step}
            )
        passed = [send(x_ref, slot(s), pass_sem.at[0], pair_sem.at[0], other)]
        for step in range(1, count):
            copies[step].wait_recv()
            passed.append(
                send(slot(s ^ step), slot(s ^ step), pass_sem.at[step], pair_sem.at[step], other)
            )
        for copy in passed:
            copy.wait()
        for step in range(1, count):
            copies[step].wait_send()
        own.wait()

    return comm_call(
        kernel,
        jax.ShapeDtypeStruct((rows * count * 2, cols), values.dtype),
        [
            pltpu.SemaphoreType.DMA((count - 1,)),
            pltpu.SemaphoreType.DMA((count - 1,)),
            pltpu.SemaphoreType.DMA((count,)),
            pltpu.SemaphoreType.DMA((count,)),
            pltpu.SemaphoreType.DMA,
        ],
        1,
        1 << 24,
        values,
    )


def plane_scatter(values, ident, after=()):
    count = lax.axis_size("shard")
    rows, cols = values.shape[0] // (count * 2), values.shape[1]
    f32 = jnp.float32
    bf = jnp.bfloat16

    def kernel(p_ref, o_ref, got, staged, arrived, pass_sem, pair_sem, send_sem, recv_sem):
        s, t = lax.axis_index("shard"), lax.axis_index("tp")
        other = {"tp": 1 - t}
        greet([other] + [{"shard": s ^ step} for step in range(1, count)])

        def chunk(index, core):
            return p_ref.at[pl.ds(pl.multiple_of((index * 2 + core) * rows, rows), rows)]

        order = list(range(count - 1, -1, -1))
        first = {}
        for step in order:
            first[step] = send(
                chunk(s ^ step, 1 - t), got.at[step], pass_sem.at[step], pair_sem.at[step], other
            )
        second = []
        for step in order:
            first[step].wait_recv()
            total = chunk(s ^ step, t)[...].astype(f32) + got[step].astype(f32)
            if step > 0:
                staged[step - 1] = total.astype(bf)
                second.append(
                    send(
                        staged.at[step - 1],
                        arrived.at[step - 1],
                        send_sem.at[step - 1],
                        recv_sem.at[step - 1],
                        {"shard": s ^ step},
                    )
                )
            else:
                o_ref[...] = total
        for copy, step in zip(second, order):
            copy.wait_recv()
            o_ref[...] += arrived[step - 1].astype(f32)
        for step in order:
            first[step].wait_send()
        for copy in second:
            copy.wait_send()

    return comm_call(
        kernel,
        jax.ShapeDtypeStruct((rows, cols), f32),
        [
            pltpu.VMEM((count, rows, cols), bf),
            pltpu.VMEM((count - 1, rows, cols), bf),
            pltpu.VMEM((count - 1, rows, cols), bf),
            pltpu.SemaphoreType.DMA((count,)),
            pltpu.SemaphoreType.DMA((count,)),
            pltpu.SemaphoreType.DMA((count - 1,)),
            pltpu.SemaphoreType.DMA((count - 1,)),
        ],
        ident,
        1 << 24,
        values.astype(bf),
        after=after,
    )


def sum_everywhere(values):
    shards, lines = lax.axis_size("shard"), lax.axis_size("ctx")
    shape = values.shape

    def kernel(x_ref, o_ref, got, staged, arrived, send_sem, recv_sem, line_send, line_recv):
        s, c, t = lax.axis_index("shard"), lax.axis_index("ctx"), lax.axis_index("tp")
        plane = [
            {"shard": s ^ step, "tp": 1 - t if swap else t}
            for step in range(shards)
            for swap in range(2)
            if step or swap
        ]
        line = [{"ctx": c ^ step} for step in range(1, lines)]
        greet(plane + line)
        copies = [
            send(x_ref, got.at[i], send_sem.at[i], recv_sem.at[i], peer)
            for i, peer in enumerate(plane)
        ]
        total = x_ref[...]
        for i, copy in enumerate(copies):
            copy.wait_recv()
            total = total + got[i]
        staged[...] = total
        o_ref[...] = total
        lines_out = [
            send(staged, arrived.at[i], line_send.at[i], line_recv.at[i], peer)
            for i, peer in enumerate(line)
        ]
        for i, copy in enumerate(lines_out):
            copy.wait_recv()
            o_ref[...] += arrived[i]
        for copy in copies + lines_out:
            copy.wait_send()

    near, far = shards * 2 - 1, lines - 1
    return comm_call(
        kernel,
        jax.ShapeDtypeStruct(shape, values.dtype),
        [
            pltpu.VMEM((near,) + shape, values.dtype),
            pltpu.VMEM(shape, values.dtype),
            pltpu.VMEM((far,) + shape, values.dtype),
            pltpu.SemaphoreType.DMA((near,)),
            pltpu.SemaphoreType.DMA((near,)),
            pltpu.SemaphoreType.DMA((far,)),
            pltpu.SemaphoreType.DMA((far,)),
        ],
        3,
        1 << 22,
        values,
    )


def swap_planes(values, count):
    pairs = [(a * count + b, b * count + a) for a in range(count) for b in range(count)]
    return lax.ppermute(values, ("shard", "ctx"), pairs)


def norm_back(values, gain, d_out):
    mean = jnp.mean(values, axis=-1, keepdims=True)
    centred = values - mean
    scale = lax.rsqrt(jnp.mean(centred * centred, axis=-1, keepdims=True) + 1e-05)
    unit = centred * scale
    d_unit = d_out * gain
    first = jnp.mean(d_unit, axis=-1, keepdims=True)
    second = jnp.mean(d_unit * unit, axis=-1, keepdims=True)
    d_values = (d_unit - first - unit * second) * scale
    return d_values, jnp.sum(d_out * unit, axis=0), jnp.sum(d_out, axis=0)


def attention(query, key, value, allowed, heads):
    f32 = jnp.float32
    parts = []
    saved = []
    for head in range(heads):
        cols = slice(head * HEAD_DIM, (head + 1) * HEAD_DIM)
        scores = lax.dot_general(
            query[:, cols], key[:, cols], (((1,), (1,)), ((), ())), preferred_element_type=f32
        )
        weights = jnp.where(allowed, jnp.exp(scores), 0.0)
        total = jnp.sum(weights, axis=1, keepdims=True)
        parts.append(dot32(weights.astype(jnp.bfloat16), value[:, cols]) / total)
        saved.append(jnp.log(total))
    return jnp.concatenate(parts, axis=1).astype(jnp.bfloat16), saved


def attention_back(query, key, value, attended, d_attended, allowed, saved, heads):
    f32 = jnp.float32
    bf = jnp.bfloat16
    d_q, d_k, d_v = [], [], []
    for head in range(heads):
        cols = slice(head * HEAD_DIM, (head + 1) * HEAD_DIM)
        q, k, v, da = query[:, cols], key[:, cols], value[:, cols], d_attended[:, cols]
        delta = jnp.sum(da.astype(f32) * attended[:, cols].astype(f32), axis=1, keepdims=True)
        scores = lax.dot_general(q, k, (((1,), (1,)), ((), ())), preferred_element_type=f32)
        probs = jnp.where(allowed, jnp.exp(scores - saved[head]), 0.0)
        d_v.append(
            lax.dot_general(
                probs.astype(bf), da, (((0,), (0,)), ((), ())), preferred_element_type=f32
            )
        )
        d_probs = lax.dot_general(da, v, (((1,), (1,)), ((), ())), preferred_element_type=f32)
        d_scores = (probs * (d_probs - delta)).astype(bf)
        d_q.append(dot32(d_scores, k))
        d_k.append(
            lax.dot_general(d_scores, q, (((0,), (0,)), ((), ())), preferred_element_type=f32)
        )
    join = lambda items: jnp.concatenate(items, axis=1)
    return join(d_q) * 0.125, join(d_k), join(d_v)


def t_dot(left, right):
    return lax.dot_general(left, right, (((0,), (0,)), ((), ())), preferred_element_type=jnp.float32)


def dot_t(left, right):
    return lax.dot_general(left, right, (((1,), (1,)), ((), ())), preferred_element_type=jnp.float32)


def on_device_plane(
    inputs,
    lengths,
    cotangent,
    w_qkv,
    w_out,
    w_fc,
    w_proj,
    b_qv,
    b_out,
    b_fc,
    b_proj,
    ln1_gain,
    ln1_bias,
    ln2_gain,
    ln2_bias,
):
    bf = jnp.bfloat16
    f32 = jnp.float32
    shards = lax.axis_size("shard")
    cores = lax.axis_size("tp")
    s = lax.axis_index("shard")
    t = lax.axis_index("tp")
    rows = inputs.shape[0] // cores
    block = rows * cores * shards
    model = inputs.shape[1]
    width = b_qv.shape[1] // shards
    heads = width // HEAD_DIM
    units = b_fc.shape[0] // shards
    mine = lambda array: lax.dynamic_slice_in_dim(array, t * rows, rows, axis=0)

    x_f = swap_planes(mine(inputs), shards).astype(f32)
    lens = swap_planes(lengths, shards)[0]
    cot_own = swap_planes(mine(cotangent), shards)
    normed1 = plane_gather(layer_norm(x_f, ln1_gain, ln1_bias).astype(bf))
    wqkv, wout, wfc, wproj = all_to_all(
        [w_qkv, w_out, w_fc, w_proj], [(2, 1), (0, 1), (1, 0), (0, 1)], 4
    )
    cot = plane_gather(cot_own)
    b_qv_own = lax.dynamic_slice_in_dim(b_qv, s * width, width, axis=1)
    b_fc_own = lax.dynamic_slice_in_dim(b_fc, s * units, units, axis=0)

    seg = segment_ids(lens, block)
    places = jnp.arange(block, dtype=jnp.int32)
    allowed = (places[None, :] <= places[:, None]) & (seg[None, :] == seg[:, None])

    query = ((dot32(normed1, wqkv[0]) + b_qv_own[0]) * 0.125).astype(bf)
    key = dot32(normed1, wqkv[1]).astype(bf)
    value = (dot32(normed1, wqkv[2]) + b_qv_own[1]).astype(bf)
    attended, saved = attention(query, key, value, allowed, heads)
    hidden = x_f + plane_scatter(dot32(attended, wout), 2) + b_out
    normed2 = plane_gather(layer_norm(hidden, ln2_gain, ln2_bias).astype(bf))
    pre = dot32(normed2, wfc) + b_fc_own
    act = gelu_tanh(pre).astype(bf)
    d_act = dot_t(cot, wproj)
    d_pre = jax.vjp(gelu_tanh, pre)[1](d_act)[0]
    d_pre_b = d_pre.astype(bf)
    g_proj = t_dot(act, cot)
    g_fc = t_dot(normed2, d_pre_b)
    early = all_to_all([g_proj.astype(bf), g_fc.astype(bf)], [(1, 0), (0, 1)], 5)
    line_parts = [
        lax.psum_scatter(moved, "ctx", scatter_dimension=0, tiled=True) for moved in early
    ]
    d_normed2 = plane_scatter(dot_t(d_pre_b, wfc), 7, (early[0],))
    g_bfc = jnp.sum(d_pre, axis=0)

    cot_f = cot_own.astype(f32)
    d_norm2, g_ln2g, g_ln2b = norm_back(hidden, ln2_gain, d_normed2)
    d_hidden = cot_f + d_norm2
    d_hidden_b = plane_gather(d_hidden.astype(bf))
    g_out = t_dot(attended, d_hidden_b)
    d_attended = dot_t(d_hidden_b, wout).astype(bf)
    d_query, d_key, d_value = attention_back(
        query, key, value, attended, d_attended, allowed, saved, heads
    )
    d_query_b, d_key_b, d_value_b = d_query.astype(bf), d_key.astype(bf), d_value.astype(bf)
    g_qkv = jnp.stack([t_dot(normed1, d_query_b), t_dot(normed1, d_key_b), t_dot(normed1, d_value_b)])
    held = [hold(line_parts[0], d_hidden_b), hold(line_parts[1], d_query_b)]
    late = all_to_all(
        [g_out.astype(bf), g_qkv.astype(bf)], [(1, 0), (1, 2)], 6, tuple(held)
    )
    d_normed1 = plane_scatter(
        dot_t(d_query_b, wqkv[0]) + dot_t(d_key_b, wqkv[1]) + dot_t(d_value_b, wqkv[2]),
        8,
        (late[0],),
    )
    d_norm1, g_ln1g, g_ln1b = norm_back(x_f, ln1_gain, d_normed1)
    grad_inputs = (d_hidden + d_norm1).astype(bf)

    def home(values):
        return lax.all_gather(swap_planes(values, shards), "tp", axis=0, tiled=True)

    mlp_total = plane_scatter(dot32(act, wproj), 9, (d_normed1,))
    outputs = (hidden + mlp_total + b_proj).astype(bf)
    sum_proj, sum_fc = [
        lax.all_gather(part, "ctx", axis=0, tiled=True).astype(f32) for part in held
    ]
    sum_out = lax.psum(late[0], "ctx").astype(f32)
    sum_qkv = lax.psum(late[1], "ctx").astype(f32)
    col = t * b_qv.shape[1] + s * width
    g_bqv = jnp.stack([jnp.sum(d_query, axis=0), jnp.sum(d_value, axis=0)])
    full_bqv = lax.dynamic_update_slice(jnp.zeros((2, b_qv.shape[1] * cores), f32), g_bqv, (0, col))
    full_bfc = lax.dynamic_update_slice(
        jnp.zeros((b_fc.shape[0] * cores,), f32), g_bfc, (t * b_fc.shape[0] + s * units,)
    )
    packed = jnp.concatenate(
        [
            full_bqv.reshape(-1),
            full_bfc,
            jnp.sum(d_hidden, axis=0),
            jnp.sum(cot_f, axis=0),
            g_ln1g,
            g_ln1b,
            g_ln2g,
            g_ln2b,
        ]
    )
    packed = sum_everywhere(packed.reshape(-1, 128)).reshape(-1)
    at = full_bqv.size
    sum_bqv = lax.dynamic_slice_in_dim(
        packed[:at].reshape(full_bqv.shape), t * b_qv.shape[1], b_qv.shape[1], axis=1
    )
    sum_bfc = lax.dynamic_slice_in_dim(packed, at + t * b_fc.shape[0], b_fc.shape[0])
    at = at + full_bfc.size
    rest = packed[at:].reshape(6, model)
    return (
        home(outputs),
        home(grad_inputs),
        sum_qkv,
        sum_out,
        sum_fc,
        sum_proj,
        sum_bqv,
        rest[0],
        sum_bfc,
        rest[1],
        rest[2],
        rest[3],
        rest[4],
        rest[5],
    )


def solution(mesh):
    in_specs = (
        P(("shard", "ctx"), None),
        P("shard", None),
        P(("shard", "ctx"), None),
        P(None, "shard", "tp"),
        P("tp", "shard"),
        P("shard", "tp"),
        P("tp", "shard"),
        P(None, "tp"),
        P(),
        P("tp"),
        P(),
        P(),
        P(),
        P(),
        P(),
    )
    out_specs = (
        P(("shard", "ctx"), None),
        P(("shard", "ctx"), None),
        P(None, "shard", "tp"),
        P("tp", "shard"),
        P("shard", "tp"),
        P("tp", "shard"),
        P(None, "tp"),
        P(),
        P("tp"),
        P(),
        P(),
        P(),
        P(),
        P(),
    )
    count = mesh.shape["shard"]
    square = count == mesh.shape["ctx"] and count & (count - 1) == 0 and mesh.shape["tp"] == 2
    body = on_device_plane if square else on_device_general
    return jax.shard_map(
        body, mesh=mesh, in_specs=in_specs, out_specs=out_specs, check_vma=False
    )
```
